128 devices in a mesh: gy: 32 (over y, x, core), gx: 4 (over z).
Axes of the slice: x: 4, y: 4, z: 4, core: 2. Of those that a mesh axis runs over, the one named last changes fastest.
Arguments:
- velocity: bfloat16 [3, 32, 1536, 1536], P(None, 'gy', 'gx'), may hold values from -40 to 40
- ref_planes: int32 [6], replicated, may hold values from 4 to 27, as said below
- partner_offsets: int32 [8], replicated, may hold values from -4 to 4, as said below
- band_owner: int32 [48], replicated, may hold values from 0 to 31, as said below
Outputs:
- correlations: float32 [96, 9, 384, 384], P('gy', None, 'gx')
The draws below stay inside these ranges and needn't reach their ends.
Inputs may be any that keep to these rules, and one draw needn't show every extreme that they name: `ref_planes`: 6 distinct planes; 4 and 27 are among them. `partner_offsets`: 8 distinct offsets; -4 and 4 are among them. `band_owner`: the pairs owned by one index of gy are consecutive; no index owns more than 3 pairs and one owns exactly 3.
All inputs are finite; a program needn't handle non-finite values.
Results may differ from the reference program's by a relative error of at most 0.0035.
Values may be sent and summed in bfloat16 or wider, within the bound.
No kernel may reach another device: no remote copies, remote signals or barrier semaphores. Data moves between devices by JAX's collectives and lax.ppermute only.
A program may use at most 128 MiB of HBM per device.

```python
import math
import jax
import jax.numpy as jnp
from jax import lax

NX = 1536
NZ = 1536
NY = 32
NREF = 6
NOFF = 8
PAIRS = 48
SLOTS = 3
LX = 384
LZ = 384
N_GY = 32


def bridge_along(noise, axis, length):
    summed = jnp.cumsum(noise, axis=axis)
    last = jnp.take(summed, jnp.array([length - 1]), axis=axis)
    shape = [1] * noise.ndim
    shape[axis] = length
    ramp = ((jnp.arange(length, dtype=jnp.float32) + 1.0) / length).reshape(shape)
    return jnp.clip((summed - ramp * last) / math.sqrt(length) * 2.0, -6.0, 6.0)


def draw_velocity(key, part):
    key_noise = jax.random.fold_in(key, 11)
    key_fresh = jax.random.fold_in(key, 12)
    key_wave = jax.random.fold_in(key, 13)
    key_amp = jax.random.fold_in(key, 14)
    key_phase = jax.random.fold_in(key, 16)
    memory = 0.75
    renew = math.sqrt(1.0 - memory * memory)
    waves = jax.random.randint(key_wave, (NY,), 2, 10).astype(jnp.float32)
    phases = jax.random.uniform(key_phase, (NY,), jnp.float32, -math.pi, math.pi)
    span_pos = jnp.arange(NZ, dtype=jnp.float32)
    amplitude = jax.random.uniform(key_amp, (NY, 3, 1, 1), jnp.float32, 0.5, 1.5)

    def fresh(plane_index):
        plane_key = jax.random.fold_in(key_fresh, plane_index)
        streak = bridge_along(jax.random.normal(jax.random.fold_in(plane_key, 1), (3, NX, NZ), jnp.float32), 1, NX)
        spanwise = bridge_along(jax.random.normal(jax.random.fold_in(plane_key, 2), (3, NX, NZ), jnp.float32), 2, NZ)
        modulation = 1.0 + 0.8 * jnp.cos(2.0 * math.pi * waves[plane_index] * span_pos / NZ + phases[plane_index])
        return streak * modulation[None, None, :] + spanwise

    def plane_noise(plane_index):
        noise_key = jax.random.fold_in(key_noise, plane_index)
        return jax.random.truncated_normal(noise_key, -5.0, 5.0, (3, NX, NZ), jnp.float32)

    def advance(shared, plane_index):
        shared = jnp.where(plane_index == 0, fresh(plane_index), jnp.clip(memory * shared + renew * fresh(plane_index), -12.0, 12.0))
        field = plane_noise(plane_index) + amplitude[plane_index] * shared
        return (shared, field.astype(jnp.bfloat16))
    start = jnp.zeros((3, NX, NZ), jnp.float32)
    final, planes = lax.scan(advance, start, jnp.arange(NY, dtype=jnp.int32))
    return planes.transpose(1, 0, 2, 3)


def draw_ref_planes(key, part):
    key_pick = jax.random.fold_in(key, 21)
    key_order = jax.random.fold_in(key, 22)
    inner = jax.random.permutation(key_pick, NY - 10) + 5
    chosen = jnp.concatenate([jnp.array([4, NY - 5], dtype=jnp.int32), inner[:NREF - 2].astype(jnp.int32)])
    return jax.random.permutation(key_order, chosen).astype(jnp.int32)


def draw_partner_offsets(key, part):
    key_drop = jax.random.fold_in(key, 31)
    key_order = jax.random.fold_in(key, 32)
    dropped = jax.random.randint(key_drop, (), -3, 4)
    values = jnp.arange(8, dtype=jnp.int32) - 4
    values = values + (values >= dropped).astype(jnp.int32)
    return jax.random.permutation(key_order, values).astype(jnp.int32)


def draw_band_owner(key, part):
    key_caps = jax.random.fold_in(key, 41)
    key_order = jax.random.fold_in(key, 42)
    lowest = (SLOTS + 1) // 2
    capacity = jax.random.randint(key_caps, (N_GY,), lowest, SLOTS + 1)
    device_order = jax.random.permutation(key_order, N_GY).astype(jnp.int32)
    ordered_caps = capacity[device_order].at[0].set(SLOTS)
    band_ends = jnp.cumsum(ordered_caps)
    positions = jnp.arange(PAIRS, dtype=jnp.int32)
    position_band = jnp.sum((band_ends[None, :] <= positions[:, None]).astype(jnp.int32), axis=1)
    position_band = jnp.minimum(position_band, N_GY - 1)
    return device_order[position_band].astype(jnp.int32)


def setup_inputs(seed: int = 0) -> dict:
    splits = jax.random.split(jax.random.key(seed), 5)
    return {
        "velocity": draw_velocity(jax.random.fold_in(splits[4], 71), 0),
        "ref_planes": draw_ref_planes(jax.random.fold_in(splits[4], 71), 0),
        "partner_offsets": draw_partner_offsets(jax.random.fold_in(splits[4], 71), 0),
        "band_owner": draw_band_owner(jax.random.fold_in(splits[4], 71), 0),
    }


def angle_table(count_rows, count_cols, length):
    rows = jnp.arange(count_rows, dtype=jnp.int32)
    cols = jnp.arange(count_cols, dtype=jnp.int32)
    phase = (rows[:, None] * cols[None, :]) % length
    return (2.0 * math.pi / length) * phase.astype(jnp.float32)


def reference(velocity, ref_planes, partner_offsets, band_owner):
    half = NZ // 2
    z_angle = angle_table(NZ, half, NZ)
    forward_z = jnp.concatenate([jnp.cos(z_angle), -jnp.sin(z_angle)], axis=1).astype(jnp.bfloat16)
    x_angle = angle_table(NX, NX, NX)
    cos_x = jnp.cos(x_angle).astype(jnp.bfloat16)
    sin_x = jnp.sin(x_angle).astype(jnp.bfloat16)
    lag_angle_x = angle_table(LX, LX, LX)
    cos_lag = jnp.cos(lag_angle_x)
    sin_lag = jnp.sin(lag_angle_x)
    lag_angle_z = angle_table(LZ, LZ, LZ)
    cos_span = jnp.cos(lag_angle_z)
    sin_span = jnp.sin(lag_angle_z)
    norm_scale = 1.0 / float(NX * NZ) ** 2
    highest = lax.Precision.HIGHEST

    def spectrum(plane_index):
        plane = lax.dynamic_index_in_dim(velocity, plane_index, 1, keepdims=False)
        along_z = jnp.dot(plane.reshape(3 * NX, NZ), forward_z, preferred_element_type=jnp.float32).astype(jnp.bfloat16)
        columns = along_z.reshape(3, NX, NZ).transpose(1, 0, 2).reshape(NX, 3 * NZ)
        cosine_part = jnp.dot(cos_x, columns, preferred_element_type=jnp.float32).reshape(NX, 3, 2, half)
        sine_part = jnp.dot(sin_x, columns, preferred_element_type=jnp.float32).reshape(NX, 3, 2, half)
        real_part = cosine_part[:, :, 0] + sine_part[:, :, 1]
        imag_part = cosine_part[:, :, 1] - sine_part[:, :, 0]
        return jnp.stack([real_part, imag_part])

    spectra = lax.map(spectrum, jnp.arange(NY, dtype=jnp.int32))
    weight = jnp.where(jnp.arange(half, dtype=jnp.int32) == 0, 1.0, 2.0).astype(jnp.float32)

    def pair_lags(pair_index):
        ref_index = ref_planes[pair_index // NOFF]
        other_index = ref_index + partner_offsets[pair_index % NOFF]
        left = spectra[ref_index] * weight
        right = spectra[other_index]
        prod_real = left[0][:, :, None, :] * right[0][:, None, :, :] + left[1][:, :, None, :] * right[1][:, None, :, :]
        prod_imag = left[0][:, :, None, :] * right[1][:, None, :, :] - left[1][:, :, None, :] * right[0][:, None, :, :]
        fold_real = prod_real.reshape(4, LX, 3, 3, 2, LZ).sum(axis=(0, 4))
        fold_imag = prod_imag.reshape(4, LX, 3, 3, 2, LZ).sum(axis=(0, 4))
        lag_real = jnp.einsum('ka,kijz->ijaz', cos_lag, fold_real, precision=highest) - jnp.einsum('ka,kijz->ijaz', sin_lag, fold_imag, precision=highest)
        lag_imag = jnp.einsum('ka,kijz->ijaz', sin_lag, fold_real, precision=highest) + jnp.einsum('ka,kijz->ijaz', cos_lag, fold_imag, precision=highest)
        lagged = jnp.einsum('ijaz,zb->ijab', lag_real, cos_span, precision=highest) - jnp.einsum('ijaz,zb->ijab', lag_imag, sin_span, precision=highest)
        return (lagged * norm_scale).reshape(9, LX, LZ)

    results = lax.map(pair_lags, jnp.arange(PAIRS, dtype=jnp.int32))
    pair_order = jnp.arange(PAIRS, dtype=jnp.int32)
    same_owner = band_owner[:, None] == band_owner[None, :]
    earlier = pair_order[None, :] < pair_order[:, None]
    slot_of = jnp.sum((same_owner & earlier).astype(jnp.int32), axis=1).astype(jnp.int32)
    dest_row = (band_owner * SLOTS + slot_of).astype(jnp.int32)
    output = jnp.zeros((SLOTS * N_GY, 9, LX, LZ), jnp.float32)
    return output.at[dest_row].set(results)
```

```python
import math

import jax
import jax.numpy as jnp
import numpy as np
from jax import lax
from jax.experimental import pallas as pl
from jax.experimental.pallas import tpu as pltpu
from jax.sharding import Mesh, PartitionSpec as P

NX = 1536
NZ = 1536
LAG = 384
NY = 32
REFS = 6
OFFS = 8
PAIRS = REFS * OFFS
SLOTS = 3
CHIPS = 64
DEVICES = 128
QB = 96
F32 = jnp.float32
BF16 = jnp.bfloat16
VMEM_BYTES = 60 * 1024 * 1024


def modes_of(chip, core):
    out = []
    for k in range(3):
        j = 3 * chip + k
        if core == 0:
            out.append(j)
        else:
            out.append(LAG // 2 if j == 0 else LAG - j)
    return out


def z_table():
    z = np.arange(NZ)
    rows = []
    for gy in range(32):
        for gx in range(4):
            kzs = modes_of((gy // 2) * 4 + gx, gy % 2)
            six = kzs + [k + LAG for k in kzs]
            order = [(0, 0), (0, 1), (0, 2), (0, 3), (0, 4), (0, 5), (1, 4), (1, 5), (1, 0), (1, 1), (1, 2), (1, 3)]
            for part, pos in order:
                angle = 2.0 * math.pi / NZ * ((six[pos] * z) % NZ)
                rows.append(np.cos(angle) if part == 0 else -np.sin(angle))
    return np.stack(rows).astype(np.float32)


def x_table():
    out = np.zeros((4, 2, LAG, 2, 4, 128), np.float64)
    x = np.arange(LAG)[:, None]
    lane = np.arange(QB)[None, :]
    for r in range(4):
        for m in range(4):
            angle = 2.0 * math.pi / NX * ((x * (4 * (lane + QB * m) + r)) % NX)
            out[r, 0, :, 0, m, :QB] = np.cos(angle)
            out[r, 1, :, 0, m, :QB] = np.sin(angle)
            out[r, 0, :, 1, m, :QB] = -np.sin(angle)
            out[r, 1, :, 1, m, :QB] = np.cos(angle)
    return out.reshape(4, 2 * LAG, 1024).astype(np.float32)


def x_lag_table():
    out = np.zeros((2, 4, 128, 4, 128), np.float64)
    lane = np.arange(QB)[:, None]
    col = np.arange(QB)[None, :]
    for r in range(4):
        for g in range(4):
            angle = 2.0 * math.pi / LAG * (((4 * lane + r) * (QB * g + col)) % LAG)
            out[0, r, :QB, g, :QB] = np.cos(angle)
            out[1, r, :QB, g, :QB] = -np.sin(angle)
    return out.reshape(1024, 512).astype(np.float32)


def z_lag_table():
    out = np.zeros((CHIPS, 8, LAG), np.float64)
    t = np.arange(LAG)
    for chip in range(CHIPS):
        for k in range(3):
            j = 3 * chip + k
            if j == 0:
                out[chip, k] = (1.0 + (-1.0) ** t) / 2.0
                out[chip, 3 + k] = (1.0 - (-1.0) ** t) / 2.0
            else:
                angle = 2.0 * math.pi / LAG * ((j * t) % LAG)
                out[chip, k] = np.cos(angle)
                out[chip, 3 + k] = -np.sin(angle)
    return out.reshape(CHIPS * 8, LAG).astype(np.float32)


def z_kernel(table_ref, vel_ref, out_ref):
    dests = out_ref.shape[0]
    for c in range(3):
        acc = lax.dot_general(
            table_ref[...], vel_ref[c], (((1,), (1,)), ((), ())), preferred_element_type=F32
        )
        for d in range(dests):
            for t in range(3):
                row = 12 * d + 4 * t
                out_ref[d, t, :, c * LAG : (c + 1) * LAG] = acc[row : row + 4].astype(BF16)


def z_transform(table, vel):
    block = 16
    return pl.pallas_call(
        z_kernel,
        grid=(DEVICES // block,),
        in_specs=[
            pl.BlockSpec((12 * block, NZ), lambda i: (i, 0)),
            pl.BlockSpec((3, LAG, NZ), lambda i: (0, 0, 0)),
        ],
        out_specs=pl.BlockSpec((block, 3, 4, 3 * LAG), lambda i: (i, 0, 0, 0)),
        out_shape=jax.ShapeDtypeStruct((DEVICES, 3, 4, 3 * LAG), BF16),
        compiler_params=pltpu.CompilerParams(vmem_limit_bytes=VMEM_BYTES),
        name="z_transform",
    )(table, vel)


def mid_kernel(
    planes_ref, order_ref, arr_ref, wx_ref, tx_ref, coef_ref, send_ref, keep_ref, lhs_ref, u_ref, prod_ref, res_ref
):
    def butterfly(i, carry):
        pieces = [[] for _ in range(4)]
        for yy in range(2):
            for c in range(3):
                re, im = [], []
                for g in range(4):
                    src = (2 * i + yy) * 4 + g
                    lanes = slice(c * LAG, (c + 1) * LAG)
                    t0 = arr_ref[src, 0, :, lanes].astype(F32)
                    t1 = arr_ref[src, 1, :, lanes].astype(F32)
                    t2 = arr_ref[src, 2, :, lanes].astype(F32)
                    re.append(jnp.concatenate([t0, t1], axis=0))
                    im.append(jnp.concatenate([t2, t1[2:4], t1[0:2]], axis=0))
                s02r, d02r = re[0] + re[2], re[0] - re[2]
                s02i, d02i = im[0] + im[2], im[0] - im[2]
                s13r, d13r = re[1] + re[3], re[1] - re[3]
                s13i, d13i = im[1] + im[3], im[1] - im[3]
                parts = [
                    (s02r + s13r, s02i + s13i),
                    (d02r + d13i, d02i - d13r),
                    (s02r - s13r, s02i - s13i),
                    (d02r - d13i, d02i + d13r),
                ]
                for r in range(4):
                    pieces[r].append(parts[r])
        for r in range(4):
            for h in range(3):
                lo, hi = pieces[r][2 * h], pieces[r][2 * h + 1]
                row = pl.multiple_of(i * 48 + 16 * h, 16)
                for part in range(2):
                    both = jnp.concatenate([lo[part], hi[part]], axis=0).astype(BF16)
                    lhs_ref[r, pl.ds(row, 16), part * LAG : (part + 1) * LAG] = both
        return carry

    lax.fori_loop(0, NY // 2, butterfly, 0)

    def transform(r, carry):
        for tile in range(4):
            out = jnp.dot(
                lhs_ref[r], wx_ref[r, :, tile * 256 : (tile + 1) * 256], preferred_element_type=F32
            )
            u_ref[r, 2 * tile] = out[:, :128].reshape(3 * NY, 8, 128)
            u_ref[r, 2 * tile + 1] = out[:, 128:].reshape(3 * NY, 8, 128)
        return carry

    lax.fori_loop(0, 4, transform, 0)

    alpha = coef_ref[0]
    beta = coef_ref[1]
    weight = coef_ref[2]
    low = lax.broadcasted_iota(jnp.int32, (8, 128), 0) < 3

    def fold(x):
        x = x * weight
        return x + jnp.where(low, pltpu.roll(x, 5, 0), pltpu.roll(x, 3, 0))

    def ref_group(ref, carry):
        first = planes_ref[ref] * 3

        def pair_products(o, inner):
            second = (planes_ref[ref] + planes_ref[REFS + o]) * 3
            for r in range(4):
                acc_re = [None] * 9
                acc_im = [None] * 9
                for m in range(4):
                    ar = [u_ref[r, m, first + i] for i in range(3)]
                    ai = [u_ref[r, 4 + m, first + i] for i in range(3)]
                    br = [u_ref[r, m, second + j] for j in range(3)]
                    bi = [u_ref[r, 4 + m, second + j] for j in range(3)]
                    for i in range(3):
                        for j in range(3):
                            re = ar[i] * br[j] + ai[i] * bi[j]
                            im = ar[i] * bi[j] - ai[i] * br[j]
                            ij = 3 * i + j
                            acc_re[ij] = re if m == 0 else acc_re[ij] + re
                            acc_im[ij] = im if m == 0 else acc_im[ij] + im
                for ij in range(9):
                    re = fold(acc_re[ij])
                    im = fold(acc_im[ij])
                    row = o * 9 + ij
                    prod_ref[row, :, r * 128 : (r + 1) * 128] = alpha * re + beta * im
                    prod_ref[row, :, 512 + r * 128 : 512 + (r + 1) * 128] = alpha * im - beta * re
            return inner

        lax.fori_loop(0, OFFS, pair_products, 0)
        lhs = prod_ref[...].reshape(OFFS * 72, 1024).astype(BF16)
        out = jnp.dot(lhs, tx_ref[...], preferred_element_type=F32)
        res_ref[pl.ds(ref * 72, 72)] = out.reshape(OFFS * 9, 8, 512)
        return carry

    lax.fori_loop(0, REFS, ref_group, 0)
    res_ref[pl.ds(PAIRS * 9, 9)] = jnp.zeros((9, 8, 512), F32)

    lane = lax.broadcasted_iota(jnp.int32, (8, 128), 1)

    def pack(base, out_ref):
        def owner(o, carry):
            at = [order_ref[base + o * SLOTS + s] * 9 for s in range(SLOTS)]
            for g in range(4):
                for group in range(7):
                    count = 4 if group < 6 else 3
                    piece = []
                    for n in range(count):
                        f = 4 * group + n
                        v = res_ref[at[f // 9] + f % 9, :, g * 128 : (g + 1) * 128]
                        piece.append(pltpu.roll(v, 96 * n % 128, 1) if n else v)
                    v0 = jnp.where(lane < 96, piece[0], piece[1])
                    v1 = jnp.where(lane < 64, piece[1], piece[2])
                    if count == 4:
                        v2 = jnp.where(lane < 32, piece[2], piece[3])
                    else:
                        v2 = jnp.where(lane < 32, piece[2], 0.0)
                    wide = jnp.concatenate([v0, v1, v2], axis=1).astype(BF16)
                    out_ref[o, g, :, group * 384 : (group + 1) * 384] = wide
            return carry

        lax.fori_loop(0, 16, owner, 0)

    pack(0, send_ref)
    pack(16 * SLOTS, keep_ref)


def middle(planes, order, arr, wx, tx, coef):
    shape = jax.ShapeDtypeStruct((16, 4, 8, 2688), BF16)
    vmem = pl.BlockSpec(memory_space=pltpu.VMEM)
    smem = pl.BlockSpec(memory_space=pltpu.SMEM)
    return pl.pallas_call(
        mid_kernel,
        in_specs=[smem, smem, vmem, vmem, vmem, vmem],
        out_specs=[vmem, vmem],
        out_shape=[shape, shape],
        scratch_shapes=[
            pltpu.VMEM((4, 24 * NY, 2 * LAG), BF16),
            pltpu.VMEM((4, 8, 3 * NY, 8, 128), F32),
            pltpu.VMEM((OFFS * 9, 8, 1024), F32),
            pltpu.VMEM(((PAIRS + 1) * 9, 8, 512), F32),
        ],
        compiler_params=pltpu.CompilerParams(vmem_limit_bytes=VMEM_BYTES),
        name="middle",
    )(planes, order, arr, wx, tx, coef)


def lag_kernel(x_ref, hi_ref, lo_ref, out_ref):
    dims = (((0,), (0,)), ((), ()))
    x = x_ref[...]
    acc = lax.dot_general(x, hi_ref[...], dims, preferred_element_type=F32)
    acc = acc + lax.dot_general(x, lo_ref[...], dims, preferred_element_type=F32)
    out_ref[...] = acc * (2.0 / float(NX * NZ) ** 2)


def z_lags(x, hi, lo):
    return pl.pallas_call(
        lag_kernel,
        grid=(7,),
        in_specs=[
            pl.BlockSpec((CHIPS * 8, 384), lambda i: (0, i)),
            pl.BlockSpec((CHIPS * 8, LAG), lambda i: (0, 0)),
            pl.BlockSpec((CHIPS * 8, LAG), lambda i: (0, 0)),
        ],
        out_specs=pl.BlockSpec((384, LAG), lambda i: (i, 0)),
        out_shape=jax.ShapeDtypeStruct((SLOTS * 9 * QB, LAG), F32),
        compiler_params=pltpu.CompilerParams(vmem_limit_bytes=VMEM_BYTES),
        name="z_lags",
    )(x, hi, lo)


def per_device(velocity, ref_planes, partner_offsets, band_owner):
    core = lax.axis_index("core")
    first_chip = (lax.axis_index("y") == 0) & (lax.axis_index("x") == 0) & (lax.axis_index("z") == 0)

    forward_z = jnp.asarray(z_table()).astype(BF16)
    parcels = z_transform(forward_z, velocity.reshape(3, LAG, NZ))
    arrived = lax.all_to_all(parcels, ("y", "x", "core", "z"), split_axis=0, concat_axis=0, tiled=True)

    pair = jnp.arange(PAIRS, dtype=jnp.int32)
    same = band_owner[:, None] == band_owner[None, :]
    slot = jnp.sum((same & (pair[None, :] < pair[:, None])).astype(jnp.int32), axis=1)
    dest = band_owner * SLOTS + slot
    hit = dest[None, :] == jnp.arange(32 * SLOTS, dtype=jnp.int32)[:, None]
    table = PAIRS + jnp.sum(jnp.where(hit, pair[None, :] - PAIRS, 0), axis=1)
    table = table.reshape(16, 2, SLOTS)
    order = jnp.where(
        core == 0,
        jnp.concatenate([table[:, 1], table[:, 0]]),
        jnp.concatenate([table[:, 0], table[:, 1]]),
    ).reshape(-1)

    row = jnp.arange(8, dtype=jnp.int32)
    sign = jnp.where(core == 0, 1.0, -1.0)
    special = first_chip & (row == 3)
    odd = row >= 3
    alpha = jnp.where(odd, jnp.where(special, sign, 0.0), 1.0)
    beta = jnp.where(odd & ~special, sign, 0.0)
    weight = jnp.where(first_chip & (core == 0) & (row == 0), 0.5, 1.0)
    coef = jnp.broadcast_to(jnp.stack([alpha, beta, weight])[:, :, None], (3, 8, 128)).astype(F32)

    send, keep = middle(
        jnp.concatenate([ref_planes, partner_offsets]),
        order,
        arrived,
        jnp.asarray(x_table()).astype(BF16),
        jnp.asarray(x_lag_table()).astype(BF16),
        coef,
    )
    other = lax.ppermute(send, "core", [(0, 1), (1, 0)])
    folded = (keep.astype(F32) + other.astype(F32)).astype(BF16).reshape(CHIPS, 8, 2688)
    spread = lax.all_to_all(folded, ("y", "x", "z"), split_axis=0, concat_axis=0, tiled=True)
    full = jnp.asarray(z_lag_table())
    hi = full.astype(BF16)
    lo = (full - hi.astype(F32)).astype(BF16)
    lags = z_lags(spread.reshape(CHIPS * 8, 2688), hi, lo)
    return lags.reshape(SLOTS, 9, QB, LAG)


def solution(mesh):
    inner = Mesh(mesh.devices.reshape(4, 4, 2, 4), ("y", "x", "core", "z"))
    gy = ("y", "x", "core")
    return jax.shard_map(
        per_device,
        mesh=inner,
        in_specs=(P(None, gy, "z", None), P(), P(), P()),
        out_specs=P(gy, None, "z", None),
        check_vma=False,
    )
```

```python
import math

import jax
import jax.numpy as jnp
import numpy as np
from jax import lax
from jax.experimental import pallas as pl
from jax.experimental.pallas import tpu as pltpu
from jax.sharding import Mesh, PartitionSpec as P

NX = 1536
NZ = 1536
LAG = 384
NY = 32
REFS = 6
OFFS = 8
PAIRS = REFS * OFFS
SLOTS = 3
CHIPS = 64
DEVICES = 128
QB = 96
F32 = jnp.float32
BF16 = jnp.bfloat16
WIDE = 1408
VMEM_BYTES = 60 * 1024 * 1024


def modes_of(chip, core):
    out = []
    for k in range(3):
        j = 3 * chip + k
        if core == 0:
            out.append(j)
        else:
            out.append(LAG // 2 if j == 0 else LAG - j)
    return out


def z_table():
    z = np.arange(NZ)
    order = [(0, 0), (0, 1), (0, 2), (1, 3), (0, 3), (0, 4), (0, 5), (1, 4), (1, 0), (1, 1), (1, 2), (1, 5)]
    rows = []
    for gy in range(32):
        for gx in range(4):
            core = gy % 2
            kzs = modes_of((gy // 2) * 4 + gx, core)
            six = kzs + [k + LAG for k in kzs]
            sign = 1.0 if core == 0 else -1.0
            for part, pos in order:
                angle = 2.0 * math.pi / NZ * ((six[pos] * z) % NZ)
                rows.append(np.cos(angle) if part == 0 else -sign * np.sin(angle))
    return np.stack(rows).astype(np.float32)


def x_table():
    out = np.zeros((4, 2, LAG, 2, 4, 128), np.float64)
    x = np.arange(LAG)[:, None]
    lane = np.arange(QB)[None, :]
    for r in range(4):
        for m in range(4):
            angle = 2.0 * math.pi / NX * ((x * (4 * (lane + QB * m) + r)) % NX)
            out[r, 0, :, 0, m, :QB] = np.cos(angle)
            out[r, 1, :, 0, m, :QB] = np.sin(angle)
            out[r, 0, :, 1, m, :QB] = -np.sin(angle)
            out[r, 1, :, 1, m, :QB] = np.cos(angle)
    return out.reshape(4, 2 * LAG, 4, 256).transpose(2, 0, 1, 3).astype(np.float32)


def x_lag_table():
    out = np.zeros((2, 4, QB, 4, 128), np.float64)
    q = np.arange(QB)[:, None]
    col = np.arange(QB)[None, :]
    for r in range(4):
        for g in range(4):
            angle = 2.0 * math.pi / LAG * (((4 * q + r) * (QB * g + col)) % LAG)
            out[0, r, :, g, :QB] = np.cos(angle)
            out[1, r, :, g, :QB] = -np.sin(angle)
    return out.reshape(2 * LAG, 512).astype(np.float32)


def z_lag_table():
    out = np.zeros((CHIPS, 6, LAG), np.float64)
    t = np.arange(LAG)
    for chip in range(CHIPS):
        for k in range(3):
            j = 3 * chip + k
            if j == 0:
                out[chip, k] = (1.0 + (-1.0) ** t) / 2.0
                out[chip, 3 + k] = (1.0 - (-1.0) ** t) / 2.0
            else:
                angle = 2.0 * math.pi / LAG * ((j * t) % LAG)
                out[chip, k] = np.cos(angle)
                out[chip, 3 + k] = -np.sin(angle)
    return out.reshape(CHIPS * 6, LAG).astype(np.float32)


def z_kernel(table_ref, vel_ref, out_ref):
    half = NZ // 2
    for part in range(2):
        acc = lax.dot_general(
            table_ref[part * half : (part + 1) * half],
            vel_ref[0],
            (((1,), (1,)), ((), ())),
            preferred_element_type=F32,
        )
        for d in range(DEVICES // 2):
            for t in range(3):
                row = 12 * d + 4 * t
                out_ref[part * (DEVICES // 2) + d, 0, t] = acc[row : row + 4].astype(BF16)


def z_transform(table, vel):
    return pl.pallas_call(
        z_kernel,
        grid=(3,),
        in_specs=[
            pl.BlockSpec((NZ, NZ), lambda c: (0, 0)),
            pl.BlockSpec((1, LAG, NZ), lambda c: (c, 0, 0)),
        ],
        out_specs=pl.BlockSpec((DEVICES, 1, 3, 4, LAG), lambda c: (0, c, 0, 0, 0)),
        out_shape=jax.ShapeDtypeStruct((DEVICES, 3, 3, 4, LAG), BF16),
        compiler_params=pltpu.CompilerParams(vmem_limit_bytes=VMEM_BYTES),
        name="z_transform",
    )(table, vel)


def side_by_side(pieces, lane):
    rolled = [pltpu.roll(v, 96 * n % 128, 1) if n else v for n, v in enumerate(pieces)]
    out = [jnp.where(lane < 96, rolled[0], rolled[1])]
    if len(pieces) == 2:
        return out + [jnp.where(lane < 64, rolled[1], 0.0)]
    out.append(jnp.where(lane < 64, rolled[1], rolled[2]))
    out.append(jnp.where(lane < 32, rolled[2], rolled[3]))
    return out


def product_kernel(planes_ref, arr_ref, wx_ref, coef_ref, send_ref, keep_ref, lhs_ref, tmp_ref, u_ref):
    core = planes_ref[REFS + OFFS]
    scale = coef_ref[...]

    def butterfly(i, carry):
        pieces = [[] for _ in range(4)]
        for yy in range(2):
            for c in range(3):
                comp = jnp.where(core == 0, c, 2 - c)
                re, im = [], []
                for g in range(4):
                    src = (2 * i + yy) * 4 + g
                    t0 = arr_ref[src, comp, 0].astype(F32)
                    t1 = arr_ref[src, comp, 1].astype(F32)
                    t2 = arr_ref[src, comp, 2].astype(F32)
                    re.append(jnp.concatenate([t0[0:3], t0[0:1], t1[0:3], t1[0:1]], axis=0))
                    im.append(
                        jnp.concatenate([t2[0:3], t2[0:1], t0[3:4], t1[3:4], t2[3:4], t0[3:4]], axis=0)
                    )
                s02r, d02r = re[0] + re[2], re[0] - re[2]
                s02i, d02i = im[0] + im[2], im[0] - im[2]
                s13r, d13r = re[1] + re[3], re[1] - re[3]
                s13i, d13i = im[1] + im[3], im[1] - im[3]
                parts = [
                    (s02r + s13r, s02i + s13i),
                    (d02r + d13i, d02i - d13r),
                    (s02r - s13r, s02i - s13i),
                    (d02r - d13i, d02i + d13r),
                ]
                for r in range(4):
                    pieces[r].append([part * scale for part in parts[r]])
        for r in range(4):
            for h in range(3):
                lo, hi = pieces[r][2 * h], pieces[r][2 * h + 1]
                row = pl.multiple_of(i * 48 + 16 * h, 16)
                for part in range(2):
                    both = jnp.concatenate([lo[part], hi[part]], axis=0).astype(BF16)
                    lhs_ref[r, pl.ds(row, 16), part * LAG : (part + 1) * LAG] = both
        return carry

    lax.fori_loop(0, NY // 2, butterfly, 0)

    lane = lax.broadcasted_iota(jnp.int32, (8, 128), 1)

    def transform(tile, carry):
        for r in range(4):
            out = jnp.dot(lhs_ref[r], wx_ref[tile, r], preferred_element_type=F32)
            tmp_ref[r] = out.reshape(3 * NY, 8, 256)

        def merge(n, inner):
            for k in range(4):
                row = 4 * n + k
                for h in range(2):
                    v = side_by_side([tmp_ref[r, row, :, h * 128 : (h + 1) * 128] for r in range(4)], lane)
                    u_ref[2 * tile + h, row] = jnp.concatenate(v, axis=1)
            return inner

        lax.fori_loop(0, 3 * NY // 4, merge, 0)
        return carry

    lax.fori_loop(0, 4, transform, 0)

    low = lax.broadcasted_iota(jnp.int32, (8, 128), 0) < 4

    def pair_products(p, carry):
        plane = planes_ref[p // OFFS]
        first = plane * 3
        second = (plane + planes_ref[REFS + p % OFFS]) * 3
        for lg in range(3):
            at = slice(lg * 128, (lg + 1) * 128)
            sums = [None] * 27
            for m in range(4):
                ar = [u_ref[m, first + i, :, at] for i in range(3)]
                ai = [u_ref[4 + m, first + i, :, at] for i in range(3)]
                br = [u_ref[m, second + j, :, at] for j in range(3)]
                bi = [u_ref[4 + m, second + j, :, at] for j in range(3)]
                ad = [ar[i] - ai[i] for i in range(3)]
                bs = [br[j] + bi[j] for j in range(3)]
                for i in range(3):
                    for j in range(3):
                        n = 3 * (3 * i + j)
                        for q, term in enumerate((ar[i] * br[j], ai[i] * bi[j], ad[i] * bs[j])):
                            sums[n + q] = term if m == 0 else sums[n + q] + term
            for ij in range(9):
                rr, ii, mixed = sums[3 * ij : 3 * ij + 3]
                re = rr + ii
                im = mixed + (ii - rr)
                folded = jnp.where(low, re, im) + pltpu.roll(jnp.where(low, im, re), 4, 0)
                if ij <= 4:
                    keep_ref[p, ij, :, at] = folded
                if ij >= 4:
                    send_ref[p, 8 - ij, :, at] = folded
        return carry

    lax.fori_loop(0, PAIRS, pair_products, 0)


def products(planes, arr, wx, coef):
    shape = jax.ShapeDtypeStruct((PAIRS, 5, 8, LAG), F32)
    vmem = pl.BlockSpec(memory_space=pltpu.VMEM)
    smem = pl.BlockSpec(memory_space=pltpu.SMEM)
    return pl.pallas_call(
        product_kernel,
        in_specs=[smem, vmem, vmem, vmem],
        out_specs=[vmem, vmem],
        out_shape=[shape, shape],
        scratch_shapes=[
            pltpu.VMEM((4, 24 * NY, 2 * LAG), BF16),
            pltpu.VMEM((4, 3 * NY, 8, 256), F32),
            pltpu.VMEM((8, 3 * NY, 8, LAG), F32),
        ],
        compiler_params=pltpu.CompilerParams(vmem_limit_bytes=VMEM_BYTES),
        name="products",
    )(planes, arr, wx, coef)


def x_lag_kernel(order_ref, keep_ref, other_ref, tx_ref, coef_ref, out_ref, res_ref):
    ref = pl.program_id(0)
    total = keep_ref[...] * coef_ref[0] + other_ref[...] * coef_ref[1]
    total = total.reshape(OFFS * 5 * 8, LAG)
    swap = coef_ref[2] > 0.5
    sign = coef_ref[3]
    rows = OFFS * 5
    halves = [[], []]
    for n in range(rows):
        x = total[8 * n : 8 * n + 8]
        halves[0].append(jnp.where(swap, pltpu.roll(x, 1, 0), x))
        halves[1].append(jnp.where(swap, pltpu.roll(x, 5, 0), pltpu.roll(x, 4, 0) * sign))
    lhs = jnp.concatenate([jnp.concatenate(h, axis=0) for h in halves], axis=1).astype(BF16)
    out = jnp.dot(lhs, tx_ref[...], preferred_element_type=F32)
    low = lax.broadcasted_iota(jnp.int32, (8, 512), 0) < 3
    for n in range(rows):
        x = out[8 * n : 8 * n + 8]
        res_ref[ref * rows + n] = jnp.where(low, x, pltpu.roll(x, 7, 0))

    @pl.when(ref == REFS - 1)
    def _():
        res_ref[PAIRS * 5 : PAIRS * 5 + 5] = jnp.zeros((5, 8, 512), F32)
        core = order_ref[32 * SLOTS]
        lane = lax.broadcasted_iota(jnp.int32, (8, 128), 1)

        def owner(o, carry):
            at = [order_ref[o * SLOTS + s] * 5 for s in range(SLOTS)]
            index = [at[f // 4] + f % 4 for f in range(12)]
            index.append(jnp.where(core == 0, at[0], at[1]) + 4)
            index.append(jnp.where(core == 0, at[2] + 4, PAIRS * 5))
            for g in range(4):
                for group in range(4):
                    pick = index[4 * group : 4 * group + 4]
                    v = side_by_side([res_ref[n, :, g * 128 : (g + 1) * 128] for n in pick], lane)
                    wide = jnp.concatenate(v, axis=1)
                    for t in range(3):
                        out_ref[o * 4 + g, t, :, group * 384 : group * 384 + 128 * len(v)] = wide[
                            2 * t : 2 * t + 2
                        ].astype(BF16)
            return carry

        lax.fori_loop(0, 32, owner, 0)


def x_lags(order, keep, other, tx, coef):
    block = pl.BlockSpec((OFFS, 5, 8, LAG), lambda i: (i, 0, 0, 0))
    return pl.pallas_call(
        x_lag_kernel,
        grid=(REFS,),
        in_specs=[
            pl.BlockSpec(memory_space=pltpu.SMEM),
            block,
            block,
            pl.BlockSpec((2 * LAG, 512), lambda i: (0, 0)),
            pl.BlockSpec((4, 8, LAG), lambda i: (0, 0, 0)),
        ],
        out_specs=pl.BlockSpec((DEVICES, 3, 2, WIDE), lambda i: (0, 0, 0, 0)),
        out_shape=jax.ShapeDtypeStruct((DEVICES, 3, 2, WIDE), BF16),
        scratch_shapes=[pltpu.VMEM(((PAIRS + 1) * 5, 8, 512), F32)],
        compiler_params=pltpu.CompilerParams(vmem_limit_bytes=VMEM_BYTES),
        name="x_lags",
    )(order, keep, other, tx, coef)


def z_lag_kernel(x_ref, hi_ref, lo_ref, out_ref, full_ref):
    core = pl.program_id(0)

    def gather(i, carry):
        x = x_ref[pl.ds(8 * i, 8)].astype(F32)
        rows = jnp.concatenate([x[c, t] for c in range(8) for t in range(3)], axis=0)
        full_ref[pl.ds(pl.multiple_of(48 * i, 16), 48), :] = rows.astype(BF16)
        return carry

    lax.fori_loop(0, CHIPS // 8, gather, 0)
    dims = (((0,), (0,)), ((), ()))
    for group in range(4):
        count = 4 if group < 3 else 2
        x = full_ref[:, group * 384 : group * 384 + (384 if group < 3 else 256)]
        acc = lax.dot_general(x, hi_ref[...], dims, preferred_element_type=F32)
        acc = acc + lax.dot_general(x, lo_ref[...], dims, preferred_element_type=F32)
        acc = acc * (2.0 / float(NX * NZ) ** 2)
        for n in range(count):
            plane = acc[QB * n : QB * n + QB]
            if group < 3:
                ij = jnp.where(core == 0, n, 8 - n)
                out_ref[group, ij] = plane
            elif n == 0:
                out_ref[core, 4] = plane
            else:

                @pl.when(core == 0)
                def _():
                    out_ref[2, 4] = plane


def z_lags(x, hi, lo):
    return pl.pallas_call(
        z_lag_kernel,
        grid=(2,),
        in_specs=[
            pl.BlockSpec((CHIPS, 3, 2, WIDE), lambda i: (i, 0, 0, 0)),
            pl.BlockSpec((CHIPS * 6, LAG), lambda i: (0, 0)),
            pl.BlockSpec((CHIPS * 6, LAG), lambda i: (0, 0)),
        ],
        out_specs=pl.BlockSpec((SLOTS, 9, QB, LAG), lambda i: (0, 0, 0, 0)),
        out_shape=jax.ShapeDtypeStruct((SLOTS, 9, QB, LAG), F32),
        scratch_shapes=[pltpu.VMEM((CHIPS * 6, WIDE), BF16)],
        compiler_params=pltpu.CompilerParams(vmem_limit_bytes=VMEM_BYTES),
        name="z_lags",
    )(x, hi, lo)


def per_device(velocity, ref_planes, partner_offsets, band_owner):
    core = lax.axis_index("core").astype(jnp.int32)
    first_chip = (lax.axis_index("y") == 0) & (lax.axis_index("x") == 0) & (lax.axis_index("z") == 0)

    forward_z = jnp.asarray(z_table()).astype(BF16)
    parcels = z_transform(forward_z, velocity.reshape(3, LAG, NZ))
    arrived = lax.all_to_all(parcels, ("y", "x", "core", "z"), split_axis=0, concat_axis=0, tiled=True)

    pair = jnp.arange(PAIRS, dtype=jnp.int32)
    same = band_owner[:, None] == band_owner[None, :]
    slot = jnp.sum((same & (pair[None, :] < pair[:, None])).astype(jnp.int32), axis=1)
    dest = ((band_owner % 2) * 16 + band_owner // 2) * SLOTS + slot
    hit = dest[None, :] == jnp.arange(32 * SLOTS, dtype=jnp.int32)[:, None]
    table = PAIRS + jnp.sum(jnp.where(hit, pair[None, :] - PAIRS, 0), axis=1)
    order = jnp.concatenate([table, core[None]])

    row = jnp.arange(8, dtype=jnp.int32)
    sign = jnp.where(core == 0, 1.0, -1.0)
    extra = row % 4 == 3
    halved = first_chip & (core == 0) & ((row == 0) | (row == 3))
    scale = jnp.broadcast_to(jnp.where(halved, math.sqrt(0.5), 1.0)[:, None], (8, LAG)).astype(F32)
    coef = jnp.stack(
        [
            jnp.where(extra, sign, 1.0),
            jnp.where(extra, -sign, 1.0),
            jnp.where(first_chip & (row == 4), 1.0, 0.0),
            jnp.where(row < 4, 1.0, -1.0),
        ]
    )
    coef = jnp.broadcast_to(coef[:, :, None], (4, 8, LAG)).astype(F32)

    send, keep = products(
        jnp.concatenate([ref_planes, partner_offsets, core[None]]),
        arrived,
        jnp.asarray(x_table()).astype(BF16),
        scale,
    )
    other = lax.ppermute(send, "core", [(0, 1), (1, 0)])
    spread = x_lags(order, keep, other, jnp.asarray(x_lag_table()).astype(BF16), coef)
    landed = lax.all_to_all(spread, ("core", "y", "x", "z"), split_axis=0, concat_axis=0, tiled=True)
    full = jnp.asarray(z_lag_table())
    hi = full.astype(BF16)
    lo = (full - hi.astype(F32)).astype(BF16)
    return z_lags(landed, hi, lo)


def solution(mesh):
    inner = Mesh(mesh.devices.reshape(4, 4, 2, 4), ("y", "x", "core", "z"))
    gy = ("y", "x", "core")
    return jax.shard_map(
        per_device,
        mesh=inner,
        in_specs=(P(None, gy, "z", None), P(), P(), P()),
        out_specs=P(gy, None, "z", None),
        check_vma=False,
    )
```

```python
import math

import jax
import jax.numpy as jnp
import numpy as np
from jax import lax
from jax.experimental import pallas as pl
from jax.experimental.pallas import tpu as pltpu
from jax.sharding import Mesh, PartitionSpec as P

NX = 1536
NZ = 1536
LAG = 384
NY = 32
REFS = 6
OFFS = 8
PAIRS = REFS * OFFS
SLOTS = 3
CHIPS = 64
DEVICES = 128
QB = 96
F32 = jnp.float32
BF16 = jnp.bfloat16
WIDE = 1408
STEP = 8
MIB = 1024 * 1024


def fold_of(chip, k):
    quarter = CHIPS // 4
    if chip < 2 * quarter:
        return 12 * (chip % quarter) + 4 * k + 2 * (chip // quarter)
    return 6 * (chip - 2 * quarter) + 2 * k + 1


def modes_of(chip, core):
    out = []
    for k in range(3):
        j = fold_of(chip, k)
        if core == 0:
            out.append(j)
        else:
            out.append(LAG // 2 if j == 0 else LAG - j)
    return out


def z_table():
    z = np.arange(NZ // 2)
    order = [(0, 0), (0, 1), (0, 2), (1, 3), (0, 3), (0, 4), (0, 5), (1, 4), (1, 0), (1, 1), (1, 2), (1, 5)]
    rows = []
    for gy in range(32):
        for gx in range(4):
            core = gy % 2
            kzs = modes_of((gy // 2) * 4 + gx, core)
            six = kzs + [k + LAG for k in kzs]
            sign = 1.0 if core == 0 else -1.0
            for part, pos in order:
                angle = 2.0 * math.pi / NZ * ((six[pos] * z) % NZ)
                rows.append(np.cos(angle) if part == 0 else -sign * np.sin(angle))
    return np.stack(rows).astype(np.float32)


def x_table():
    out = np.zeros((4, 2, LAG, 2, 4, 128), np.float64)
    x = np.arange(LAG)[:, None]
    lane = np.arange(QB)[None, :]
    for r in range(4):
        for m in range(4):
            angle = 2.0 * math.pi / NX * ((x * (4 * (lane + QB * m) + r)) % NX)
            out[r, 0, :, 0, m, :QB] = np.cos(angle)
            out[r, 1, :, 0, m, :QB] = np.sin(angle)
            out[r, 0, :, 1, m, :QB] = -np.sin(angle)
            out[r, 1, :, 1, m, :QB] = np.cos(angle)
    return out.reshape(4, 2 * LAG, 4, 256).transpose(2, 0, 1, 3).astype(np.float32)


def x_lag_table():
    out = np.zeros((2, 4, QB, 4, 128), np.float64)
    q = np.arange(QB)[:, None]
    col = np.arange(QB)[None, :]
    for r in range(4):
        for g in range(4):
            angle = 2.0 * math.pi / LAG * (((4 * q + r) * (QB * g + col)) % LAG)
            out[0, r, :, g, :QB] = np.cos(angle)
            out[1, r, :, g, :QB] = -np.sin(angle)
    return out.reshape(2 * LAG, 512).astype(np.float32)


def z_lag_table():
    out = np.zeros((CHIPS, 6, LAG), np.float64)
    t = np.arange(LAG)
    for chip in range(CHIPS):
        for k in range(3):
            j = fold_of(chip, k)
            if j == 0:
                out[chip, k] = (1.0 + (-1.0) ** t) / 2.0
                out[chip, 3 + k] = (1.0 - (-1.0) ** t) / 2.0
            else:
                angle = 2.0 * math.pi / LAG * ((j * t) % LAG)
                out[chip, k] = np.cos(angle)
                out[chip, 3 + k] = -np.sin(angle)
    return out.reshape(CHIPS * 6, LAG).astype(np.float32)


def z_kernel(table_ref, vel_ref, out_ref, sum_ref, twist_ref, odd_ref):
    step = pl.program_id(0)
    quarter = NZ // 4
    first = lax.broadcasted_iota(jnp.int32, (4, LAG), 0) == 0

    def part(n):
        return vel_ref[:, :, n * quarter : (n + 1) * quarter].reshape(3 * LAG, quarter)

    def emit(field_ref, special):
        acc = lax.dot_general(
            table_ref[:, : field_ref.shape[1]],
            field_ref[...],
            (((1,), (1,)), ((), ())),
            preferred_element_type=F32,
        )
        for d in range(DEVICES // 4):
            for t in range(3):
                row = 12 * d + 4 * t
                for c in range(3):
                    piece = acc[row : row + 4, c * LAG : (c + 1) * LAG]
                    if special and d == 0 and t != 1:
                        piece = jnp.where(first, piece * math.sqrt(0.5), piece)
                    out_ref[d, c, t] = piece.astype(BF16)

    @pl.when(step == 0)
    def _():
        for c in range(3):
            q = [vel_ref[c, :, n * quarter : (n + 1) * quarter].astype(F32) for n in range(4)]
            even, other = q[0] + q[2], q[1] + q[3]
            sum_ref[c * LAG : (c + 1) * LAG] = (even + other).astype(BF16)
            twist_ref[c * LAG : (c + 1) * LAG] = (even - other).astype(BF16)
        emit(sum_ref, True)

    @pl.when(step == 1)
    def _():
        emit(twist_ref, False)

    @pl.when(step == 2)
    def _():
        odd_ref[:, :quarter] = part(0) - part(2)
        odd_ref[:, quarter:] = part(1) - part(3)

    @pl.when(step >= 2)
    def _():
        emit(odd_ref, False)


def z_transform(table, vel):
    return pl.pallas_call(
        z_kernel,
        grid=(4,),
        in_specs=[
            pl.BlockSpec((NZ // 4, NZ // 2), lambda i: (i, 0)),
            pl.BlockSpec((3, LAG, NZ), lambda i: (0, 0, 0)),
        ],
        out_specs=pl.BlockSpec((DEVICES // 4, 3, 3, 4, LAG), lambda i: (i, 0, 0, 0, 0)),
        out_shape=jax.ShapeDtypeStruct((DEVICES, 3, 3, 4, LAG), BF16),
        scratch_shapes=[
            pltpu.VMEM((3 * LAG, NZ // 4), BF16),
            pltpu.VMEM((3 * LAG, NZ // 4), BF16),
            pltpu.VMEM((3 * LAG, NZ // 2), BF16),
        ],
        compiler_params=pltpu.CompilerParams(vmem_limit_bytes=60 * MIB),
        name="z_transform",
    )(table, vel)


def side_by_side(pieces, lane):
    rolled = [pltpu.roll(v, 96 * n % 128, 1) if n else v for n, v in enumerate(pieces)]
    out = [jnp.where(lane < 96, rolled[0], rolled[1])]
    if len(pieces) == 2:
        return out + [jnp.where(lane < 64, rolled[1], 0.0)]
    out.append(jnp.where(lane < 64, rolled[1], rolled[2]))
    out.append(jnp.where(lane < 32, rolled[2], rolled[3]))
    return out


def pair_loop(planes_ref, u_ref, out_ref, kept):
    low = lax.broadcasted_iota(jnp.int32, (8, 128), 0) < 4
    chosen = range(5) if kept else range(8, 3, -1)

    def pair_products(p, carry):
        plane = planes_ref[p // OFFS]
        first = plane * 3
        second = (plane + planes_ref[REFS + p % OFFS]) * 3
        for lg in range(3):
            at = slice(lg * 128, (lg + 1) * 128)
            sums = {}
            for m in range(4):
                left, right = {}, {}
                for i in sorted({ij // 3 for ij in chosen}):
                    re, im = u_ref[m, first + i, :, at], u_ref[4 + m, first + i, :, at]
                    left[i] = (re, im, re - im)
                for j in range(3):
                    re, im = u_ref[m, second + j, :, at], u_ref[4 + m, second + j, :, at]
                    right[j] = (re, im, re + im)
                for ij in chosen:
                    terms = [a * b for a, b in zip(left[ij // 3], right[ij % 3])]
                    sums[ij] = terms if m == 0 else [s + t for s, t in zip(sums[ij], terms)]
            for n, ij in enumerate(chosen):
                rr, ii, mixed = sums[ij]
                re = rr + ii
                im = mixed + (ii - rr)
                out_ref[p, n, :, at] = jnp.where(low, re, im) + pltpu.roll(jnp.where(low, im, re), 4, 0)
        return carry

    lax.fori_loop(0, PAIRS, pair_products, 0)


def keep_kernel(planes_ref, u_ref, keep_ref):
    pair_loop(planes_ref, u_ref, keep_ref, True)


def send_kernel(planes_ref, arr_ref, wx_hbm, send_ref, u_ref, wx_ref, sem, lhs_ref, tmp0_ref, tmp1_ref):
    fetch = pltpu.make_async_copy(wx_hbm, wx_ref, sem)
    fetch.start()
    core = planes_ref[REFS + OFFS]

    def butterfly(i, carry):
        pieces = [[] for _ in range(4)]
        for yy in range(2):
            for c in range(3):
                comp = jnp.where(core == 0, c, 2 - c)
                re, im = [], []
                for g in range(4):
                    src = (2 * i + yy) * 4 + g
                    t0 = arr_ref[src, comp, 0].astype(F32)
                    t1 = arr_ref[src, comp, 1].astype(F32)
                    t2 = arr_ref[src, comp, 2].astype(F32)
                    re.append(jnp.concatenate([t0, t1], axis=0))
                    im.append(jnp.concatenate([t2, t0[3:4], t1[3:4], t2[3:4], t2[3:4]], axis=0))
                s02r, d02r = re[0] + re[2], re[0] - re[2]
                s02i, d02i = im[0] + im[2], im[0] - im[2]
                s13r, d13r = re[1] + re[3], re[1] - re[3]
                s13i, d13i = im[1] + im[3], im[1] - im[3]
                parts = [
                    (s02r + s13r, s02i + s13i),
                    (d02r + d13i, d02i - d13r),
                    (s02r - s13r, s02i - s13i),
                    (d02r - d13i, d02i + d13r),
                ]
                for r in range(4):
                    pieces[r].append(parts[r])
        for r in range(4):
            for h in range(3):
                lo, hi = pieces[r][2 * h], pieces[r][2 * h + 1]
                row = pl.multiple_of(i * 48 + 16 * h, 16)
                for part in range(2):
                    both = jnp.concatenate([lo[part], hi[part]], axis=0).astype(BF16)
                    lhs_ref[r, pl.ds(row, 16), part * LAG : (part + 1) * LAG] = both
        return carry

    lax.fori_loop(0, NY // 2, butterfly, 0)

    lane = lax.broadcasted_iota(jnp.int32, (8, 128), 1)

    fetch.wait()
    tmp = (tmp0_ref, tmp1_ref)
    for tile in range(5):
        for r in range(4):
            if tile < 4:
                out = jnp.dot(lhs_ref[r], wx_ref[tile, r], preferred_element_type=F32)
                tmp[tile % 2][r] = out.reshape(3 * NY, 8, 256)
            if tile > 0:
                done = tmp[(tile - 1) % 2]
                for row in range(24 * r, 24 * r + 24):
                    for h in range(2):
                        v = side_by_side([done[q, row, :, h * 128 : (h + 1) * 128] for q in range(4)], lane)
                        u_ref[2 * tile - 2 + h, row] = jnp.concatenate(v, axis=1)

    pair_loop(planes_ref, u_ref, send_ref, False)


def send_products(planes, arr, wx):
    vmem = pl.BlockSpec(memory_space=pltpu.VMEM)
    return pl.pallas_call(
        send_kernel,
        in_specs=[pl.BlockSpec(memory_space=pltpu.SMEM), vmem, pl.BlockSpec(memory_space=pltpu.HBM)],
        out_specs=[vmem, vmem],
        out_shape=[
            jax.ShapeDtypeStruct((PAIRS, 5, 8, LAG), F32),
            jax.ShapeDtypeStruct((8, 3 * NY, 8, LAG), F32),
        ],
        scratch_shapes=[
            pltpu.VMEM((4, 4, 2 * LAG, 256), BF16),
            pltpu.SemaphoreType.DMA,
            pltpu.VMEM((4, 24 * NY, 2 * LAG), BF16),
            pltpu.VMEM((4, 3 * NY, 8, 256), F32),
            pltpu.VMEM((4, 3 * NY, 8, 256), F32),
        ],
        compiler_params=pltpu.CompilerParams(vmem_limit_bytes=28 * MIB),
        name="send_products",
    )(planes, arr, wx)


def keep_products(planes, u):
    vmem = pl.BlockSpec(memory_space=pltpu.VMEM)
    return pl.pallas_call(
        keep_kernel,
        in_specs=[pl.BlockSpec(memory_space=pltpu.SMEM), vmem],
        out_specs=vmem,
        out_shape=jax.ShapeDtypeStruct((PAIRS, 5, 8, LAG), F32),
        cost_estimate=pl.CostEstimate(flops=60_000_000, bytes_accessed=12_000_000, transcendentals=0),
        compiler_params=pltpu.CompilerParams(vmem_limit_bytes=8 * MIB),
        name="keep_products",
    )(planes, u)


def x_lag_kernel(order_ref, keep_ref, other_ref, tx_ref, coef_ref, out_ref, res_ref):
    rows = STEP * 5
    swap = coef_ref[0] > 0.5
    sign = coef_ref[1]
    mirror = coef_ref[2]
    low = lax.broadcasted_iota(jnp.int32, (8, 512), 0) < 3

    def group(i, carry):
        halves = [[], []]
        for n in range(rows):
            mine = keep_ref[i * STEP + n // 5, n % 5]
            theirs = other_ref[i * STEP + n // 5, n % 5]
            total = mine + theirs
            apart = (mine - theirs) * mirror
            halves[0].append(jnp.where(swap, pltpu.roll(apart, 4, 0), total))
            halves[1].append(jnp.where(swap, apart, pltpu.roll(total, 4, 0) * sign))
        lhs = jnp.concatenate([jnp.concatenate(h, axis=0) for h in halves], axis=1)
        high = lhs.astype(BF16)
        rest = (lhs - high.astype(F32)).astype(BF16)
        out = jnp.dot(high, tx_ref[...], preferred_element_type=F32)
        out = out + jnp.dot(rest, tx_ref[...], preferred_element_type=F32)
        for n in range(rows):
            x = out[8 * n : 8 * n + 8]
            res_ref[i * rows + n] = jnp.where(low, x, pltpu.roll(x, 7, 0))
        return carry

    lax.fori_loop(0, PAIRS // STEP, group, 0)
    res_ref[PAIRS * 5 : PAIRS * 5 + 5] = jnp.zeros((5, 8, 512), F32)
    core = order_ref[32 * SLOTS]
    lane = lax.broadcasted_iota(jnp.int32, (8, 128), 1)

    def owner(o, carry):
        at = [order_ref[o * SLOTS + s] * 5 for s in range(SLOTS)]
        index = [at[f // 4] + f % 4 for f in range(12)]
        index.append(jnp.where(core == 0, at[0], at[1]) + 4)
        index.append(jnp.where(core == 0, at[2] + 4, PAIRS * 5))
        for g in range(4):
            for group in range(4):
                pick = index[4 * group : 4 * group + 4]
                v = side_by_side([res_ref[n, :, g * 128 : (g + 1) * 128] for n in pick], lane)
                wide = jnp.concatenate(v, axis=1)
                for t in range(3):
                    out_ref[o * 4 + g, t, :, group * 384 : group * 384 + 128 * len(v)] = wide[
                        2 * t : 2 * t + 2
                    ].astype(BF16)
        return carry

    lax.fori_loop(0, 32, owner, 0, unroll=2)


def x_lags(order, keep, other, tx, coef):
    vmem = pl.BlockSpec(memory_space=pltpu.VMEM)
    return pl.pallas_call(
        x_lag_kernel,
        in_specs=[pl.BlockSpec(memory_space=pltpu.SMEM), vmem, vmem, vmem, vmem],
        out_specs=vmem,
        out_shape=jax.ShapeDtypeStruct((DEVICES, 3, 2, WIDE), BF16),
        scratch_shapes=[pltpu.VMEM(((PAIRS + 1) * 5, 8, 512), F32)],
        compiler_params=pltpu.CompilerParams(vmem_limit_bytes=20 * MIB),
        name="x_lags",
    )(order, keep, other, tx, coef)


def z_lag_kernel(x_ref, table_ref, out_hbm, full_ref, plane_ref, sem):
    def gather(i, carry):
        x = x_ref[pl.ds(8 * i, 8)].astype(F32)
        rows = jnp.concatenate([x[c, t] for c in range(8) for t in range(3)], axis=0)
        full_ref[pl.ds(pl.multiple_of(48 * i, 16), 48), :] = rows.astype(BF16)
        return carry

    lax.fori_loop(0, 2 * CHIPS // 8, gather, 0)
    dims = (((0,), (0,)), ((), ()))
    half = CHIPS * 6

    def planes(core, group):
        stop = group * 384 + (384 if group < 3 else 256)
        x = full_ref[core * half : (core + 1) * half, group * 384 : stop]
        acc = lax.dot_general(x, table_ref[...], dims, preferred_element_type=F32)
        return acc * (2.0 / float(NX * NZ) ** 2)

    extra = planes(0, 3)
    plane_ref[0, 4] = extra[:QB]
    plane_ref[2, 4] = extra[QB : 2 * QB]
    plane_ref[1, 4] = planes(1, 3)[:QB]
    copies = []
    for slot in range(SLOTS):
        for core in range(2):
            acc = planes(core, slot)
            for n in range(4):
                plane_ref[slot, n if core == 0 else 8 - n] = acc[QB * n : QB * n + QB]
        copies.append(pltpu.make_async_copy(plane_ref.at[slot], out_hbm.at[slot], sem.at[slot]))
        copies[-1].start()
    for copy in copies:
        copy.wait()


def z_lags(x, table):
    vmem = pl.BlockSpec(memory_space=pltpu.VMEM)
    return pl.pallas_call(
        z_lag_kernel,
        in_specs=[vmem, vmem],
        out_specs=pl.BlockSpec(memory_space=pltpu.HBM),
        out_shape=jax.ShapeDtypeStruct((SLOTS, 9, QB, LAG), F32),
        scratch_shapes=[
            pltpu.VMEM((2 * CHIPS * 6, WIDE), BF16),
            pltpu.VMEM((SLOTS, 9, QB, LAG), F32),
            pltpu.SemaphoreType.DMA((SLOTS,)),
        ],
        compiler_params=pltpu.CompilerParams(vmem_limit_bytes=20 * MIB),
        name="z_lags",
    )(x, table)


def per_device(velocity, ref_planes, partner_offsets, band_owner):
    core = lax.axis_index("core").astype(jnp.int32)
    first_chip = (lax.axis_index("y") == 0) & (lax.axis_index("x") == 0) & (lax.axis_index("z") == 0)

    forward_z = jnp.asarray(z_table()).astype(BF16)
    parcels = z_transform(forward_z, velocity.reshape(3, LAG, NZ))
    arrived = lax.all_to_all(parcels, ("y", "x", "core", "z"), split_axis=0, concat_axis=0, tiled=True)

    pair = jnp.arange(PAIRS, dtype=jnp.int32)
    same = band_owner[:, None] == band_owner[None, :]
    slot = jnp.sum((same & (pair[None, :] < pair[:, None])).astype(jnp.int32), axis=1)
    dest = ((band_owner % 2) * 16 + band_owner // 2) * SLOTS + slot
    hit = dest[None, :] == jnp.arange(32 * SLOTS, dtype=jnp.int32)[:, None]
    table = PAIRS + jnp.sum(jnp.where(hit, pair[None, :] - PAIRS, 0), axis=1)
    order = jnp.concatenate([table, core[None]])

    row = jnp.arange(8, dtype=jnp.int32)
    coef = jnp.stack(
        [
            jnp.where(first_chip & (row == 4), 1.0, 0.0),
            jnp.where(row < 4, 1.0, -1.0),
            jnp.broadcast_to(jnp.where(core == 0, 1.0, -1.0), (8,)),
        ]
    )
    coef = jnp.broadcast_to(coef[:, :, None], (3, 8, LAG)).astype(F32)
    planes = jnp.concatenate([ref_planes, partner_offsets, core[None]])
    planes, order, coef, arrived = lax.optimization_barrier((planes, order, coef, arrived))

    forward_x = pltpu.with_memory_space_constraint(jnp.asarray(x_table()).astype(BF16), pltpu.HBM)
    send, spectra = send_products(planes, arrived, forward_x)
    other = lax.ppermute(send, "core", [(0, 1), (1, 0)])
    keep = keep_products(planes, spectra)
    spread = x_lags(order, keep, other, jnp.asarray(x_lag_table()).astype(BF16), coef)
    landed = lax.all_to_all(spread, ("core", "y", "x", "z"), split_axis=0, concat_axis=0, tiled=True)
    return z_lags(landed, jnp.asarray(z_lag_table()).astype(BF16))


def solution(mesh):
    inner = Mesh(mesh.devices.reshape(4, 4, 2, 4), ("y", "x", "core", "z"))
    gy = ("y", "x", "core")
    return jax.shard_map(
        per_device,
        mesh=inner,
        in_specs=(P(None, gy, "z", None), P(), P(), P()),
        out_specs=P(gy, None, "z", None),
        check_vma=False,
    )
```

```python
import math

import jax
import jax.numpy as jnp
import numpy as np
from jax import lax
from jax.experimental import pallas as pl
from jax.experimental.pallas import tpu as pltpu
from jax.sharding import Mesh, PartitionSpec as P

NX = 1536
NZ = 1536
LAG = 384
NY = 32
REFS = 6
OFFS = 8
PAIRS = REFS * OFFS
SLOTS = 3
CHIPS = 64
DEVICES = 128
QB = 96
F32 = jnp.float32
BF16 = jnp.bfloat16
WIDE = 1408
STEP = 8
MIB = 1024 * 1024


def fold_of(chip, k):
    quarter = CHIPS // 4
    if chip < 2 * quarter:
        return 12 * (chip % quarter) + 4 * k + 2 * (chip // quarter)
    return 6 * (chip - 2 * quarter) + 2 * k + 1


def modes_of(chip, core):
    out = []
    for k in range(3):
        j = fold_of(chip, k)
        if core == 0:
            out.append(j)
        else:
            out.append(LAG // 2 if j == 0 else LAG - j)
    return out


def z_table():
    z = np.arange(NZ // 2)
    order = [(0, 0), (0, 1), (0, 2), (1, 3), (0, 3), (0, 4), (0, 5), (1, 4), (1, 0), (1, 1), (1, 2), (1, 5)]
    rows = []
    for gy in range(32):
        for gx in range(4):
            core = gy % 2
            kzs = modes_of((gy // 2) * 4 + gx, core)
            six = kzs + [k + LAG for k in kzs]
            sign = 1.0 if core == 0 else -1.0
            for part, pos in order:
                angle = 2.0 * math.pi / NZ * ((six[pos] * z) % NZ)
                rows.append(np.cos(angle) if part == 0 else -sign * np.sin(angle))
    return np.stack(rows).astype(np.float32)


def x_table():
    out = np.zeros((4, 2, LAG, 2, 4, 128), np.float64)
    x = np.arange(LAG)[:, None]
    lane = np.arange(QB)[None, :]
    for r in range(4):
        for m in range(4):
            angle = 2.0 * math.pi / NX * ((x * (4 * (lane + QB * m) + r)) % NX)
            out[r, 0, :, 0, m, :QB] = np.cos(angle)
            out[r, 1, :, 0, m, :QB] = np.sin(angle)
            out[r, 0, :, 1, m, :QB] = -np.sin(angle)
            out[r, 1, :, 1, m, :QB] = np.cos(angle)
    return out.reshape(4, 2 * LAG, 4, 256).transpose(2, 0, 1, 3).astype(np.float32)


def x_lag_table():
    out = np.zeros((2, 4, QB, 4, 128), np.float64)
    q = np.arange(QB)[:, None]
    col = np.arange(QB)[None, :]
    for r in range(4):
        for g in range(4):
            angle = 2.0 * math.pi / LAG * (((4 * q + r) * (QB * g + col)) % LAG)
            out[0, r, :, g, :QB] = np.cos(angle)
            out[1, r, :, g, :QB] = -np.sin(angle)
    return out.reshape(2 * LAG, 512).astype(np.float32)


def z_lag_table():
    out = np.zeros((CHIPS, 6, LAG), np.float64)
    t = np.arange(LAG)
    for chip in range(CHIPS):
        for k in range(3):
            j = fold_of(chip, k)
            if j == 0:
                out[chip, k] = (1.0 + (-1.0) ** t) / 2.0
                out[chip, 3 + k] = (1.0 - (-1.0) ** t) / 2.0
            else:
                angle = 2.0 * math.pi / LAG * ((j * t) % LAG)
                out[chip, k] = np.cos(angle)
                out[chip, 3 + k] = -np.sin(angle)
    return out.reshape(CHIPS * 6, LAG).astype(np.float32)


def z_kernel(table_ref, vel_ref, out_ref, sum_ref, twist_ref, odd_ref):
    step = pl.program_id(0)
    quarter = NZ // 4
    first = lax.broadcasted_iota(jnp.int32, (4, LAG), 0) == 0

    def part(n):
        return vel_ref[:, :, n * quarter : (n + 1) * quarter].reshape(3 * LAG, quarter)

    def emit(field_ref, special):
        acc = lax.dot_general(
            table_ref[:, : field_ref.shape[1]],
            field_ref[...],
            (((1,), (1,)), ((), ())),
            preferred_element_type=F32,
        )
        for d in range(DEVICES // 4):
            for t in range(3):
                row = 12 * d + 4 * t
                for c in range(3):
                    piece = acc[row : row + 4, c * LAG : (c + 1) * LAG]
                    if special and d == 0 and t != 1:
                        piece = jnp.where(first, piece * math.sqrt(0.5), piece)
                    out_ref[d, c, t] = piece.astype(BF16)

    @pl.when(step == 0)
    def _():
        for c in range(3):
            q = [vel_ref[c, :, n * quarter : (n + 1) * quarter].astype(F32) for n in range(4)]
            even, other = q[0] + q[2], q[1] + q[3]
            sum_ref[c * LAG : (c + 1) * LAG] = (even + other).astype(BF16)
            twist_ref[c * LAG : (c + 1) * LAG] = (even - other).astype(BF16)
        emit(sum_ref, True)

    @pl.when(step == 1)
    def _():
        emit(twist_ref, False)

    @pl.when(step == 2)
    def _():
        odd_ref[:, :quarter] = part(0) - part(2)
        odd_ref[:, quarter:] = part(1) - part(3)

    @pl.when(step >= 2)
    def _():
        emit(odd_ref, False)


def z_transform(table, vel):
    return pl.pallas_call(
        z_kernel,
        grid=(4,),
        in_specs=[
            pl.BlockSpec((NZ // 4, NZ // 2), lambda i: (i, 0)),
            pl.BlockSpec((3, LAG, NZ), lambda i: (0, 0, 0)),
        ],
        out_specs=pl.BlockSpec((DEVICES // 4, 3, 3, 4, LAG), lambda i: (i, 0, 0, 0, 0)),
        out_shape=jax.ShapeDtypeStruct((DEVICES, 3, 3, 4, LAG), BF16),
        scratch_shapes=[
            pltpu.VMEM((3 * LAG, NZ // 4), BF16),
            pltpu.VMEM((3 * LAG, NZ // 4), BF16),
            pltpu.VMEM((3 * LAG, NZ // 2), BF16),
        ],
        compiler_params=pltpu.CompilerParams(vmem_limit_bytes=60 * MIB),
        name="z_transform",
    )(table, vel)


def side_by_side(pieces, lane):
    rolled = [pltpu.roll(v, 96 * n % 128, 1) if n else v for n, v in enumerate(pieces)]
    out = [jnp.where(lane < 96, rolled[0], rolled[1])]
    if len(pieces) == 2:
        return out + [jnp.where(lane < 64, rolled[1], 0.0)]
    out.append(jnp.where(lane < 64, rolled[1], rolled[2]))
    out.append(jnp.where(lane < 32, rolled[2], rolled[3]))
    return out


def pair_loop(planes_ref, u_ref, out_ref, kept):
    low = lax.broadcasted_iota(jnp.int32, (8, 128), 0) < 4
    chosen = range(5) if kept else range(8, 3, -1)

    def pair_products(p, carry):
        plane = planes_ref[p // OFFS]
        first = plane * 3
        second = (plane + planes_ref[REFS + p % OFFS]) * 3
        for lg in range(3):
            at = slice(lg * 128, (lg + 1) * 128)
            sums = {}
            for m in range(4):
                left, right = {}, {}
                for i in sorted({ij // 3 for ij in chosen}):
                    re, im = u_ref[m, first + i, :, at], u_ref[4 + m, first + i, :, at]
                    left[i] = (re, im, u_ref[8 + m, first + i, :, at])
                for j in range(3):
                    re, im = u_ref[m, second + j, :, at], u_ref[4 + m, second + j, :, at]
                    right[j] = (re, im, u_ref[12 + m, second + j, :, at])
                for ij in chosen:
                    terms = [a * b for a, b in zip(left[ij // 3], right[ij % 3])]
                    sums[ij] = terms if m == 0 else [s + t for s, t in zip(sums[ij], terms)]
            for n, ij in enumerate(chosen):
                rr, ii, mixed = sums[ij]
                re = rr + ii
                im = mixed + (ii - rr)
                out_ref[p, n, :, at] = jnp.where(low, re, im) + pltpu.roll(jnp.where(low, im, re), 4, 0)
        return carry

    lax.fori_loop(0, PAIRS, pair_products, 0, unroll=2)


def keep_kernel(planes_ref, u_ref, keep_ref):
    pair_loop(planes_ref, u_ref, keep_ref, True)


def send_kernel(planes_ref, arr_ref, wx_hbm, send_ref, u_ref, wx_ref, sem, lhs_ref, tmp0_ref, tmp1_ref):
    fetch = pltpu.make_async_copy(wx_hbm, wx_ref, sem)
    fetch.start()
    core = planes_ref[REFS + OFFS]

    def butterfly(i, carry):
        pieces = [[] for _ in range(4)]
        for yy in range(2):
            for c in range(3):
                comp = jnp.where(core == 0, c, 2 - c)
                re, im = [], []
                for g in range(4):
                    src = (2 * i + yy) * 4 + g
                    t0 = arr_ref[src, comp, 0].astype(F32)
                    t1 = arr_ref[src, comp, 1].astype(F32)
                    t2 = arr_ref[src, comp, 2].astype(F32)
                    re.append(jnp.concatenate([t0, t1], axis=0))
                    im.append(jnp.concatenate([t2, t0[3:4], t1[3:4], t2[3:4], t2[3:4]], axis=0))
                s02r, d02r = re[0] + re[2], re[0] - re[2]
                s02i, d02i = im[0] + im[2], im[0] - im[2]
                s13r, d13r = re[1] + re[3], re[1] - re[3]
                s13i, d13i = im[1] + im[3], im[1] - im[3]
                parts = [
                    (s02r + s13r, s02i + s13i),
                    (d02r + d13i, d02i - d13r),
                    (s02r - s13r, s02i - s13i),
                    (d02r - d13i, d02i + d13r),
                ]
                for r in range(4):
                    pieces[r].append(parts[r])
        for r in range(4):
            for h in range(3):
                lo, hi = pieces[r][2 * h], pieces[r][2 * h + 1]
                row = pl.multiple_of(i * 48 + 16 * h, 16)
                for part in range(2):
                    both = jnp.concatenate([lo[part], hi[part]], axis=0).astype(BF16)
                    lhs_ref[r, pl.ds(row, 16), part * LAG : (part + 1) * LAG] = both
        return carry

    lax.fori_loop(0, NY // 2, butterfly, 0, unroll=2)

    lane = lax.broadcasted_iota(jnp.int32, (8, 128), 1)

    fetch.wait()
    tmp = (tmp0_ref, tmp1_ref)
    for tile in range(5):
        for r in range(4):
            if tile < 4:
                out = jnp.dot(lhs_ref[r], wx_ref[tile, r], preferred_element_type=F32)
                tmp[tile % 2][r] = out.reshape(3 * NY, 8, 256)
            if tile > 0:
                done = tmp[(tile - 1) % 2]
                for row in range(24 * r, 24 * r + 24):
                    for h in range(2):
                        v = side_by_side([done[q, row, :, h * 128 : (h + 1) * 128] for q in range(4)], lane)
                        v = jnp.concatenate(v, axis=1)
                        which = 2 * tile - 2 + h
                        u_ref[which, row] = v
                        if which >= 4:
                            re = u_ref[which - 4, row]
                            u_ref[which + 4, row] = re - v
                            u_ref[which + 8, row] = re + v

    pair_loop(planes_ref, u_ref, send_ref, False)


def send_products(planes, arr, wx):
    vmem = pl.BlockSpec(memory_space=pltpu.VMEM)
    return pl.pallas_call(
        send_kernel,
        in_specs=[pl.BlockSpec(memory_space=pltpu.SMEM), vmem, pl.BlockSpec(memory_space=pltpu.HBM)],
        out_specs=[vmem, vmem],
        out_shape=[
            jax.ShapeDtypeStruct((PAIRS, 5, 8, LAG), F32),
            jax.ShapeDtypeStruct((16, 3 * NY, 8, LAG), F32),
        ],
        scratch_shapes=[
            pltpu.VMEM((4, 4, 2 * LAG, 256), BF16),
            pltpu.SemaphoreType.DMA,
            pltpu.VMEM((4, 24 * NY, 2 * LAG), BF16),
            pltpu.VMEM((4, 3 * NY, 8, 256), F32),
            pltpu.VMEM((4, 3 * NY, 8, 256), F32),
        ],
        compiler_params=pltpu.CompilerParams(vmem_limit_bytes=28 * MIB),
        name="send_products",
    )(planes, arr, wx)


def keep_products(planes, u):
    vmem = pl.BlockSpec(memory_space=pltpu.VMEM)
    return pl.pallas_call(
        keep_kernel,
        in_specs=[pl.BlockSpec(memory_space=pltpu.SMEM), vmem],
        out_specs=vmem,
        out_shape=jax.ShapeDtypeStruct((PAIRS, 5, 8, LAG), F32),
        cost_estimate=pl.CostEstimate(flops=60_000_000, bytes_accessed=22_000_000, transcendentals=0),
        compiler_params=pltpu.CompilerParams(vmem_limit_bytes=8 * MIB),
        name="keep_products",
    )(planes, u)


def x_lag_kernel(order_ref, keep_ref, other_ref, tx_ref, coef_ref, out_ref, res_ref):
    rows = STEP * 5
    swap = coef_ref[0] > 0.5
    sign = coef_ref[1]
    mirror = coef_ref[2]
    low = lax.broadcasted_iota(jnp.int32, (8, 512), 0) < 3

    def group(i, carry):
        halves = [[], []]
        for n in range(rows):
            mine = keep_ref[i * STEP + n // 5, n % 5]
            theirs = other_ref[i * STEP + n // 5, n % 5]
            total = mine + theirs
            apart = (mine - theirs) * mirror
            halves[0].append(jnp.where(swap, pltpu.roll(apart, 4, 0), total))
            halves[1].append(jnp.where(swap, apart, pltpu.roll(total, 4, 0) * sign))
        lhs = jnp.concatenate([jnp.concatenate(h, axis=0) for h in halves], axis=1)
        high = lhs.astype(BF16)
        rest = (lhs - high.astype(F32)).astype(BF16)
        out = jnp.dot(high, tx_ref[...], preferred_element_type=F32)
        out = out + jnp.dot(rest, tx_ref[...], preferred_element_type=F32)
        for n in range(rows):
            x = out[8 * n : 8 * n + 8]
            res_ref[i * rows + n] = jnp.where(low, x, pltpu.roll(x, 7, 0))
        return carry

    lax.fori_loop(0, PAIRS // STEP, group, 0)
    res_ref[PAIRS * 5 : PAIRS * 5 + 5] = jnp.zeros((5, 8, 512), F32)
    core = order_ref[32 * SLOTS]
    lane = lax.broadcasted_iota(jnp.int32, (8, 128), 1)

    def owner(o, carry):
        at = [order_ref[o * SLOTS + s] * 5 for s in range(SLOTS)]
        index = [at[f // 4] + f % 4 for f in range(12)]
        index.append(jnp.where(core == 0, at[0], at[1]) + 4)
        index.append(jnp.where(core == 0, at[2] + 4, PAIRS * 5))
        for g in range(4):
            for group in range(4):
                pick = index[4 * group : 4 * group + 4]
                v = side_by_side([res_ref[n, :, g * 128 : (g + 1) * 128] for n in pick], lane)
                wide = jnp.concatenate(v, axis=1)
                for t in range(3):
                    out_ref[o * 4 + g, t, :, group * 384 : group * 384 + 128 * len(v)] = wide[
                        2 * t : 2 * t + 2
                    ].astype(BF16)
        return carry

    lax.fori_loop(0, 32, owner, 0, unroll=2)


def x_lags(order, keep, other, tx, coef):
    vmem = pl.BlockSpec(memory_space=pltpu.VMEM)
    return pl.pallas_call(
        x_lag_kernel,
        in_specs=[pl.BlockSpec(memory_space=pltpu.SMEM), vmem, vmem, vmem, vmem],
        out_specs=vmem,
        out_shape=jax.ShapeDtypeStruct((DEVICES, 3, 2, WIDE), BF16),
        scratch_shapes=[pltpu.VMEM(((PAIRS + 1) * 5, 8, 512), F32)],
        compiler_params=pltpu.CompilerParams(vmem_limit_bytes=20 * MIB),
        name="x_lags",
    )(order, keep, other, tx, coef)


def z_lag_kernel(x_ref, table_ref, out_hbm, full_ref, plane_ref, sem):
    def gather(i, carry):
        x = x_ref[pl.ds(8 * i, 8)].astype(F32)
        rows = jnp.concatenate([x[c, t] for c in range(8) for t in range(3)], axis=0)
        full_ref[pl.ds(pl.multiple_of(48 * i, 16), 48), :] = rows.astype(BF16)
        return carry

    lax.fori_loop(0, 2 * CHIPS // 8, gather, 0)
    dims = (((0,), (0,)), ((), ()))
    half = CHIPS * 6

    def planes(core, group):
        stop = group * 384 + (384 if group < 3 else 256)
        x = full_ref[core * half : (core + 1) * half, group * 384 : stop]
        acc = lax.dot_general(x, table_ref[...], dims, preferred_element_type=F32)
        return acc * (2.0 / float(NX * NZ) ** 2)

    extra = planes(0, 3)
    plane_ref[0, 4] = extra[:QB]
    plane_ref[2, 4] = extra[QB : 2 * QB]
    plane_ref[1, 4] = planes(1, 3)[:QB]
    copies = []
    for slot in range(SLOTS):
        for core in range(2):
            acc = planes(core, slot)
            for n in range(4):
                plane_ref[slot, n if core == 0 else 8 - n] = acc[QB * n : QB * n + QB]
        copies.append(pltpu.make_async_copy(plane_ref.at[slot], out_hbm.at[slot], sem.at[slot]))
        copies[-1].start()
    for copy in copies:
        copy.wait()


def z_lags(x, table):
    vmem = pl.BlockSpec(memory_space=pltpu.VMEM)
    return pl.pallas_call(
        z_lag_kernel,
        in_specs=[vmem, vmem],
        out_specs=pl.BlockSpec(memory_space=pltpu.HBM),
        out_shape=jax.ShapeDtypeStruct((SLOTS, 9, QB, LAG), F32),
        scratch_shapes=[
            pltpu.VMEM((2 * CHIPS * 6, WIDE), BF16),
            pltpu.VMEM((SLOTS, 9, QB, LAG), F32),
            pltpu.SemaphoreType.DMA((SLOTS,)),
        ],
        compiler_params=pltpu.CompilerParams(vmem_limit_bytes=20 * MIB),
        name="z_lags",
    )(x, table)


def per_device(velocity, ref_planes, partner_offsets, band_owner):
    core = lax.axis_index("core").astype(jnp.int32)
    first_chip = (lax.axis_index("y") == 0) & (lax.axis_index("x") == 0) & (lax.axis_index("z") == 0)

    forward_z = jnp.asarray(z_table()).astype(BF16)
    parcels = z_transform(forward_z, velocity.reshape(3, LAG, NZ))
    arrived = lax.all_to_all(parcels, ("y", "x", "core", "z"), split_axis=0, concat_axis=0, tiled=True)

    pair = jnp.arange(PAIRS, dtype=jnp.int32)
    same = band_owner[:, None] == band_owner[None, :]
    slot = jnp.sum((same & (pair[None, :] < pair[:, None])).astype(jnp.int32), axis=1)
    dest = ((band_owner % 2) * 16 + band_owner // 2) * SLOTS + slot
    hit = dest[None, :] == jnp.arange(32 * SLOTS, dtype=jnp.int32)[:, None]
    table = PAIRS + jnp.sum(jnp.where(hit, pair[None, :] - PAIRS, 0), axis=1)
    order = jnp.concatenate([table, core[None]])

    row = jnp.arange(8, dtype=jnp.int32)
    coef = jnp.stack(
        [
            jnp.where(first_chip & (row == 4), 1.0, 0.0),
            jnp.where(row < 4, 1.0, -1.0),
            jnp.broadcast_to(jnp.where(core == 0, 1.0, -1.0), (8,)),
        ]
    )
    coef = jnp.broadcast_to(coef[:, :, None], (3, 8, LAG)).astype(F32)
    planes = jnp.concatenate([ref_planes, partner_offsets, core[None]])
    planes, order, coef, arrived = lax.optimization_barrier((planes, order, coef, arrived))

    forward_x = pltpu.with_memory_space_constraint(jnp.asarray(x_table()).astype(BF16), pltpu.HBM)
    send, spectra = send_products(planes, arrived, forward_x)
    other = lax.ppermute(send, "core", [(0, 1), (1, 0)])
    keep = keep_products(planes, spectra)
    spread = x_lags(order, keep, other, jnp.asarray(x_lag_table()).astype(BF16), coef)
    landed = lax.all_to_all(spread, ("core", "y", "x", "z"), split_axis=0, concat_axis=0, tiled=True)
    return z_lags(landed, jnp.asarray(z_lag_table()).astype(BF16))


def solution(mesh):
    inner = Mesh(mesh.devices.reshape(4, 4, 2, 4), ("y", "x", "core", "z"))
    gy = ("y", "x", "core")
    return jax.shard_map(
        per_device,
        mesh=inner,
        in_specs=(P(None, gy, "z", None), P(), P(), P()),
        out_specs=P(gy, None, "z", None),
        check_vma=False,
    )
```
